32 devices in a mesh: groups: 2 (over y), sec: 4 (over z), strip: 4 (over x, core).
Axes of the slice: x: 2, y: 2, z: 4, core: 2. Of those that a mesh axis runs over, the one named last changes fastest.
Arguments:
- sections: bfloat16 [4, 256, 1024], P('sec', 'strip', 'groups'), parts along dimension 2, may hold values from -40 to 40
- mask_fine: int32 [4, 8, 32], P('sec', 'strip', 'groups'), parts along dimension 2, may hold values 0 or 1
- mask_coarse: int32 [4, 4, 16], P('sec', 'strip', 'groups'), parts along dimension 2, may hold values 0 or 1
Outputs:
- corr_fine: float32 [4, 2, 8, 32, 1024], P('sec', None, 'strip', 'groups'), parts along dimension 3
- corr_coarse: float32 [4, 2, 4, 16, 1024], P('sec', None, 'strip', 'groups'), parts along dimension 3
The draws below stay inside these ranges and needn't reach their ends.
There are 2 independent parts, one for each index of `groups`. The reference program is written for one: setup_inputs(seed, part) draws one part's arguments, and reference() takes and returns one part's arrays. A program takes and returns all parts, laid end to end along the dimension named above; each array names one. Nothing has to cross between parts.
All inputs are finite; a program needn't handle non-finite values. No bound on the sum of `mask_fine` or of `mask_coarse` on one device may be relied on, other than what follows from the above.
Results may differ from the reference program's by a relative error of at most 0.0039.
Values may be sent and summed in bfloat16 or wider, within the bound.
A program may use at most 64 MiB of HBM per device.

```python
import jax
import jax.numpy as jnp
from jax import lax

PATCH = 64
STRIDE = 32
WINDOW = 32
WIDTH = 512
NZ = 4
H = 256


def draw_sections(key, part):
    key_noise, key_rows, key_cols = jax.random.split(key, 3)
    row_scale = jnp.exp(jax.random.uniform(key_rows, (NZ, H, 1), jnp.float32, 0.0, jnp.log(10.0)))
    col_scale = jnp.exp(jax.random.uniform(key_cols, (NZ, 1, WIDTH), jnp.float32, 0.0, jnp.log(10.0)))
    scaling = jnp.sqrt(row_scale * col_scale)
    section_image = jax.random.normal(key_noise, (NZ, H, WIDTH), jnp.float32) * scaling
    return jnp.clip(section_image, -40.0, 40.0).astype(jnp.bfloat16)


def set_ends(drawn, rng, low, top_value):
    index_at = [jax.random.randint(jax.random.fold_in(rng, axis), (), 0, length) for axis, length in enumerate(drawn.shape)]
    main_axis = drawn.shape.index(max(drawn.shape))
    beside = index_at[:main_axis] + [(index_at[main_axis] + 1) % drawn.shape[main_axis]] + index_at[main_axis + 1:]
    return drawn.at[tuple(index_at)].set(low).at[tuple(beside)].set(top_value)


def setup_inputs(seed: int = 0, part: int = 0) -> dict:
    splits = jax.random.split(jax.random.key(seed), 4)
    part_keys = jax.random.split(jax.random.fold_in(splits[3], part), 4)
    return {
        "sections": draw_sections(jax.random.fold_in(jax.random.fold_in(splits[3], part), 71), part),
        "mask_fine": set_ends((jax.random.randint(part_keys[1], (NZ, H // STRIDE, WIDTH // STRIDE), 0, 4) < 3).astype(jnp.int32), jax.random.fold_in(part_keys[1], 1), 0, 1),
        "mask_coarse": set_ends((jax.random.randint(part_keys[2], (NZ, H // (2 * STRIDE), WIDTH // (2 * STRIDE)), 0, 4) < 3).astype(jnp.int32), jax.random.fold_in(part_keys[2], 1), 0, 1),
    }


def make_patches(section_image, patch_rows, patch_cols):
    blocks = section_image.reshape(patch_rows + 1, STRIDE, patch_cols + 1, STRIDE)
    tall_blocks = jnp.concatenate([blocks[:-1], blocks[1:]], axis=1)
    wide_blocks = jnp.concatenate([tall_blocks[:, :, :-1], tall_blocks[:, :, 1:]], axis=3)
    return wide_blocks.transpose(1, 3, 0, 2).reshape(PATCH, PATCH, patch_rows * patch_cols)

def level_patches(extended):
    strip_rows = extended.shape[0] - PATCH
    section_width = extended.shape[1]
    fine_img = jnp.pad(extended[:strip_rows + STRIDE], ((0, 0), (0, STRIDE)))
    pooled = extended.reshape(extended.shape[0] // 2, 2, section_width // 2, 2).mean(axis=(1, 3))
    coarse_img = jnp.pad(pooled, ((0, 0), (0, STRIDE)))
    fine_patches = make_patches(fine_img, strip_rows // STRIDE, section_width // STRIDE)
    coarse_patches = make_patches(coarse_img, strip_rows // (2 * STRIDE), section_width // (2 * STRIDE))
    return jnp.concatenate([fine_patches, coarse_patches], axis=2)

def section_spectra(section_image):
    extended = jnp.pad(section_image.astype(jnp.float32), ((0, PATCH), (0, 0)))
    patches = level_patches(extended)
    centered = patches - lax.optimization_barrier(jnp.mean(patches, axis=(0, 1)))
    unit_patch = centered / jnp.sqrt(lax.optimization_barrier(jnp.mean(centered * centered, axis=(0, 1))) + 1e-05)
    spectrum = jnp.fft.fft2(unit_patch, axes=(0, 1))
    return jnp.stack([spectrum.real, spectrum.imag]).astype(jnp.bfloat16)

def window_correlation(own_spec, other_spec):
    own_spec = own_spec.astype(jnp.float32)
    other_spec = other_spec.astype(jnp.float32)
    cross_real = own_spec[0] * other_spec[0] + own_spec[1] * other_spec[1]
    cross_imag = own_spec[0] * other_spec[1] - own_spec[1] * other_spec[0]
    cross_spec = cross_real + 1j * cross_imag
    full_map = jnp.fft.ifft2(cross_spec, axes=(0, 1)).real
    shift_index = ((jnp.arange(WINDOW) - WINDOW // 2) % PATCH).astype(jnp.int32)
    picked = jnp.take(jnp.take(full_map, shift_index, axis=0), shift_index, axis=1)
    return picked / PATCH

def reference(sections, mask_fine, mask_coarse):
    spectra_all = lax.map(section_spectra, sections)
    zero_sections = jnp.zeros((2,) + spectra_all.shape[1:], spectra_all.dtype)
    padded = jnp.concatenate([spectra_all, zero_sections], axis=0)
    fine_rows = H // STRIDE
    fine_cols = WIDTH // STRIDE
    coarse_rows = H // (2 * STRIDE)
    coarse_cols = WIDTH // (2 * STRIDE)
    fine_count = fine_rows * fine_cols

    def one_section(section_items):
        own_spec, first_spec, second_spec, fine_mask, coarse_mask = section_items
        corr_maps = jnp.stack([window_correlation(own_spec, first_spec), window_correlation(own_spec, second_spec)])
        flat_maps = corr_maps.reshape(2, WINDOW * WINDOW, -1)
        fine_out = flat_maps[:, :, :fine_count].reshape(2, WINDOW * WINDOW, fine_rows, fine_cols).transpose(0, 2, 3, 1)
        coarse_out = flat_maps[:, :, fine_count:].reshape(2, WINDOW * WINDOW, coarse_rows, coarse_cols).transpose(0, 2, 3, 1)
        fine_out = fine_out * fine_mask.astype(jnp.float32)[None, :, :, None]
        coarse_out = coarse_out * coarse_mask.astype(jnp.float32)[None, :, :, None]
        return (fine_out, coarse_out)
    corr_fine, corr_coarse = lax.map(one_section, (padded[:NZ], padded[1:NZ + 1], padded[2:NZ + 2], mask_fine, mask_coarse))
    return (corr_fine, corr_coarse)
```

```python
import functools

import jax
import jax.numpy as jnp
import numpy as np
from jax import lax
from jax.experimental import pallas as pl
from jax.experimental.pallas import tpu as pltpu
from jax.sharding import PartitionSpec as P

PATCH = 64
STRIDE = 32
WINDOW = 32
HALF = PATCH // 2 + 1
KP = 40
LANES = 128
F32 = jnp.float32
BF16 = jnp.bfloat16


def shifted(value, axis, steps):
    count = lax.axis_size(axis)
    return lax.ppermute(value, axis, [(source, source - steps) for source in range(steps, count)])


def trig(phase):
    angle = 2.0 * np.pi / PATCH * np.mod(phase, PATCH)
    return np.round(np.cos(angle), 12), np.round(np.sin(angle), 12)


def split(table):
    high = np.asarray(table, np.float32).astype(BF16)
    low = (np.asarray(table, np.float64) - high.astype(np.float64)).astype(np.float32).astype(BF16)
    return high, low


def block_diagonal(block, count):
    return np.kron(np.eye(count), block)


def tables(strip_rows):
    fine_rows = strip_rows // STRIDE
    coarse_rows = strip_rows // (2 * STRIDE)
    height = strip_rows + PATCH
    k = np.arange(KP)[:, None]
    keep = (k < HALF).astype(np.float64)
    x = np.arange(height)[None, :]
    units = []
    for i in range(fine_rows):
        c, s = trig(k * (x - STRIDE * i))
        inside = ((x >= STRIDE * i) & (x < STRIDE * i + PATCH)) * keep
        units += [c * inside, -s * inside]
    for i in range(coarse_rows):
        xc = x // 2 - STRIDE * i
        c, s = trig(k * xc)
        inside = ((xc >= 0) & (xc < PATCH)) * keep * 0.25
        units += [c * inside, -s * inside]
    a_high, a_low = split(np.concatenate(units, axis=0))
    first = np.concatenate([a_high, a_low], axis=1)

    freq = np.arange(PATCH)[None, :]
    y = np.arange(STRIDE)[:, None]
    c, s = trig(y * freq)

    def second(c, s, count):
        c, s = block_diagonal(c, count), block_diagonal(s, count)
        return split(np.block([[c, -s], [s, c]]))

    fine_w = second(c, s, LANES // STRIDE)
    coarse_w = second(np.repeat(c, 2, axis=0), np.repeat(s, 2, axis=0), LANES // (2 * STRIDE))

    shift = np.arange(WINDOW) - WINDOW // 2
    c, s = trig(np.arange(PATCH)[:, None] * shift[None, :])
    c, s = block_diagonal(c, 4), block_diagonal(s, 4)
    inverse = split(np.block([[c, s], [-s, c]]))

    weight = np.where((k == 0) | (k == PATCH // 2), 1.0, 2.0) * keep
    c, s = trig(shift[:, None] * np.arange(KP)[None, :])
    last_high, last_low = split(np.concatenate([c * weight.T, -s * weight.T], axis=1))
    last = np.concatenate([last_high, last_high, last_low], axis=1)
    energy = np.kron(np.eye(4), np.ones((PATCH, WINDOW)))
    return [
        first,
        *fine_w,
        *coarse_w,
        *inverse,
        last,
        np.asarray(energy, np.float32),
        np.asarray(np.broadcast_to(weight, (KP, LANES)), np.float32),
    ]


def split_value(value):
    high = value.astype(BF16)
    return high, (value - high.astype(F32)).astype(BF16)


def matmul(a, b):
    return jnp.dot(a, b, preferred_element_type=F32)


def section_spectra(pixels, first, fine_w, coarse_w, fine_rows, coarse_rows):
    half = matmul(first, jnp.concatenate([pixels, pixels], axis=0))
    width = half.shape[1]
    tiles = width // LANES
    row = lax.broadcasted_iota(jnp.int32, (KP, width), 0)
    fine_in, coarse_in = [], []
    for unit in range(fine_rows + coarse_rows):
        real = half[2 * KP * unit : 2 * KP * unit + KP]
        imag = half[2 * KP * unit + KP : 2 * KP * (unit + 1)]
        sums = real[0:1]
        high = sums.astype(BF16).astype(F32)
        middle = (sums - high).astype(BF16).astype(F32)
        low = sums - high - middle
        real = jnp.where(row == 0, high, real)
        real = jnp.where(row == HALF, middle, real)
        real = jnp.where(row == HALF + 1, low, real)
        target = fine_in if unit < fine_rows else coarse_in
        for tile in range(tiles):
            at = slice(LANES * tile, LANES * (tile + 1))
            target.append(jnp.concatenate([real[:, at], imag[:, at]], axis=1))

    def transform(parts, weights):
        high, low = split_value(jnp.concatenate(parts, axis=0))
        w_high, w_low = weights
        return matmul(high, w_high) + matmul(low, w_high) + matmul(high, w_low)

    fine = transform(fine_in, fine_w)
    coarse = transform(coarse_in, coarse_w)
    wide = 2 * LANES
    lane = lax.broadcasted_iota(jnp.int32, (KP, wide), 1)
    krow = lax.broadcasted_iota(jnp.int32, (KP, wide), 0)
    sign = jnp.where(lane % 2 == 0, 1.0, -1.0).astype(F32)
    dc = (krow == 0) & (lane % PATCH == 0)

    def finish(parts, rows):
        count = len(parts) // rows
        rolled = [pltpu.roll(part, wide - PATCH, 1) for part in parts]
        done = []
        for index, part in enumerate(parts):
            if index % count == count - 1:
                following = jnp.where(lane < wide - PATCH, rolled[index], 0.0)
            else:
                following = jnp.where(lane < wide - PATCH, rolled[index], rolled[index + 1])
            value = part + sign * following
            value = jnp.where(krow == 0, value + value[HALF : HALF + 1] + value[HALF + 1 : HALF + 2], value)
            value = jnp.where(dc, 0.0, value)
            done.append(value)
        return done

    def groups(offset):
        fine_parts = [
            fine[KP * g : KP * (g + 1), offset * wide : (offset + 1) * wide]
            for g in range(fine_rows * tiles)
        ]
        coarse_parts = [
            jnp.concatenate(
                [
                    coarse[KP * g : KP * (g + 1), offset * LANES : (offset + 1) * LANES],
                    coarse[KP * (g + 1) : KP * (g + 2), offset * LANES : (offset + 1) * LANES],
                ],
                axis=1,
            )
            for g in range(0, coarse_rows * tiles, 2)
        ]
        return finish(fine_parts, fine_rows) + finish(coarse_parts, coarse_rows)

    return groups(0), groups(1)


def block_transpose(value):
    row = lax.broadcasted_iota(jnp.int32, value.shape, 0) % 4
    block = lax.broadcasted_iota(jnp.int32, value.shape, 1) // WINDOW
    rows = value.shape[0]
    moved = pltpu.roll(value, 2 * WINDOW, 1)
    other = jnp.where(row < 2, pltpu.roll(moved, rows - 2, 0), pltpu.roll(moved, 2, 0))
    value = jnp.where((row // 2) == (block // 2), value, other)
    right = pltpu.roll(pltpu.roll(value, WINDOW, 1), rows - 1, 0)
    left = pltpu.roll(pltpu.roll(value, LANES - WINDOW, 1), 1, 0)
    other = jnp.where(row % 2 == 0, right, left)
    return jnp.where((row % 2) == (block % 2), value, other)


def compute(
    pixels_ref,
    fine_mask_ref,
    coarse_mask_ref,
    first_ref,
    fine_high_ref,
    fine_low_ref,
    coarse_high_ref,
    coarse_low_ref,
    inverse_high_ref,
    inverse_low_ref,
    last_ref,
    energy_ref,
    weight_ref,
    fine_out_ref,
    coarse_out_ref,
    real_ref,
    imag_ref,
    sums_ref,
):
    fine_rows, fine_cols = fine_mask_ref.shape[1:]
    coarse_rows, coarse_cols = coarse_mask_ref.shape[1:]
    count = (fine_rows * fine_cols + coarse_rows * coarse_cols) // 4
    fine_groups = fine_rows * fine_cols // 4
    weight = jnp.concatenate([weight_ref[...]] * 2, axis=1)
    for section in range(3):
        real, imag = section_spectra(
            pixels_ref[section],
            first_ref[...],
            (fine_high_ref[...], fine_low_ref[...]),
            (coarse_high_ref[...], coarse_low_ref[...]),
            fine_rows,
            coarse_rows,
        )
        for g in range(count):
            real_ref[section, KP * g : KP * (g + 1)] = real[g]
            imag_ref[section, KP * g : KP * (g + 1)] = imag[g]
            power = weight * (real[g] * real[g] + imag[g] * imag[g])
            sums_ref[section, g : g + 1] = jnp.sum(power, axis=0, keepdims=True)
    scales = []
    for section in range(3):
        total = jnp.dot(
            sums_ref[section], energy_ref[...], preferred_element_type=F32, precision=lax.Precision.HIGHEST
        )
        scales.append(1.0 / jnp.sqrt(total * (1.0 / float(PATCH) ** 4) + 1e-05))

    def spread(mask, cols):
        source = lax.broadcasted_iota(jnp.int32, (cols, cols * WINDOW), 0)
        target = lax.broadcasted_iota(jnp.int32, (cols, cols * WINDOW), 1) // WINDOW
        picks = jnp.where(source == target, 1.0, 0.0).astype(BF16)
        return matmul(mask.astype(F32).astype(BF16), picks)

    fine_mask = spread(fine_mask_ref[0], fine_cols)
    coarse_mask = spread(coarse_mask_ref[0], coarse_cols)
    masks = [
        m[r : r + 1, LANES * t : LANES * (t + 1)]
        for m in (fine_mask, coarse_mask)
        for r in range(m.shape[0])
        for t in range(m.shape[1] // LANES)
    ]
    stacked = []
    for d in (1, 2):
        cross_real = real_ref[0] * real_ref[d] + imag_ref[0] * imag_ref[d]
        cross_imag = real_ref[0] * imag_ref[d] - imag_ref[0] * real_ref[d]
        cross = jnp.concatenate([cross_real.astype(BF16), cross_imag.astype(BF16)], axis=1)
        rows = matmul(cross, inverse_high_ref[...]) + matmul(cross, inverse_low_ref[...])
        for g in range(count):
            part = rows[KP * g : KP * (g + 1)]
            stacked.append(jnp.concatenate([part[:, :LANES], part[:, LANES:]], axis=0))
    high, low = split_value(jnp.concatenate(stacked, axis=1))
    maps = matmul(last_ref[...], jnp.concatenate([high, low, high], axis=0))
    for d in (1, 2):
        for g in range(count):
            scale = scales[0][g : g + 1] * scales[d][g : g + 1] * masks[g] * (1.0 / float(PATCH) ** 3)
            at = LANES * (count * (d - 1) + g)
            value = block_transpose(maps[:, at : at + LANES] * scale)
            if g < fine_groups:
                ref, local_g, cols = fine_out_ref, g, fine_cols
            else:
                ref, local_g, cols = coarse_out_ref, g - fine_groups, coarse_cols
            i, j = divmod(4 * local_g, cols)
            for q in range(WINDOW // 4):
                ref[0, d - 1, i, j : j + 4, LANES * q : LANES * (q + 1)] = value[4 * q : 4 * (q + 1)]


def local(sections, mask_fine, mask_coarse):
    strip_rows = sections.shape[1]
    near = shifted(sections, "sec", 1)
    far = shifted(sections, "sec", 2)
    own = jnp.concatenate([sections, near, far], axis=0)
    rim = shifted(own, "strip", 1)
    pixels = jnp.concatenate([own, rim], axis=1)
    consts = [jnp.asarray(t) for t in tables(strip_rows)]
    fine_rows, fine_cols = mask_fine.shape[1:]
    coarse_rows, coarse_cols = mask_coarse.shape[1:]
    count = (fine_rows * fine_cols + coarse_rows * coarse_cols) // 4
    vmem = pl.BlockSpec(memory_space=pltpu.VMEM)
    flat = WINDOW * WINDOW
    return pl.pallas_call(
        compute,
        out_shape=(
            jax.ShapeDtypeStruct((1, 2, fine_rows, fine_cols, flat), F32),
            jax.ShapeDtypeStruct((1, 2, coarse_rows, coarse_cols, flat), F32),
        ),
        in_specs=[vmem] * (3 + len(consts)),
        out_specs=(vmem, vmem),
        scratch_shapes=[
            pltpu.VMEM((3, KP * count, 2 * LANES), F32),
            pltpu.VMEM((3, KP * count, 2 * LANES), F32),
            pltpu.VMEM((3, -(-count // 8) * 8, 2 * LANES), F32),
        ],
    )(pixels, mask_fine, mask_coarse, *consts)


def solution(mesh):
    in_specs = (
        P("sec", "strip", "groups"),
        P("sec", "strip", "groups"),
        P("sec", "strip", "groups"),
    )
    out_specs = (P("sec", None, "strip", "groups", None), P("sec", None, "strip", "groups", None))
    return jax.shard_map(local, mesh=mesh, in_specs=in_specs, out_specs=out_specs, check_vma=False)
```

```python
import functools

import jax
import jax.numpy as jnp
import numpy as np
from jax import lax
from jax.experimental import pallas as pl
from jax.experimental.pallas import tpu as pltpu
from jax.sharding import PartitionSpec as P

PATCH = 64
STRIDE = 32
WINDOW = 32
HALF = PATCH // 2 + 1
KP = 40
LANES = 128
F32 = jnp.float32
BF16 = jnp.bfloat16
MESH = pl.DeviceIdType.MESH


def trig(phase):
    angle = 2.0 * np.pi / PATCH * np.mod(phase, PATCH)
    return np.round(np.cos(angle), 12), np.round(np.sin(angle), 12)


def split(table):
    high = np.asarray(table, np.float32).astype(BF16)
    low = (np.asarray(table, np.float64) - high.astype(np.float64)).astype(np.float32).astype(BF16)
    return high, low


def block_diagonal(block, count):
    return np.kron(np.eye(count), block)


def tables(strip_rows):
    fine_rows = strip_rows // STRIDE
    coarse_rows = strip_rows // (2 * STRIDE)
    height = strip_rows + PATCH
    k = np.arange(KP)[:, None]
    keep = (k < HALF).astype(np.float64)
    x = np.arange(height)[None, :]
    units = []
    for i in range(fine_rows):
        c, s = trig(k * (x - STRIDE * i))
        inside = ((x >= STRIDE * i) & (x < STRIDE * i + PATCH)) * keep
        units += [c * inside, -s * inside]
    for i in range(coarse_rows):
        xc = x // 2 - STRIDE * i
        c, s = trig(k * xc)
        inside = ((xc >= 0) & (xc < PATCH)) * keep * 0.25
        units += [c * inside, -s * inside]
    a_high, a_low = split(np.concatenate(units, axis=0))
    first = np.concatenate([a_high, a_low], axis=1)

    freq = np.arange(PATCH)[None, :]
    y = np.arange(STRIDE)[:, None]
    c, s = trig(y * freq)

    def second(c, s, count):
        c, s = block_diagonal(c, count), block_diagonal(s, count)
        return split(np.block([[c, -s], [s, c]]))

    fine_w = second(c, s, LANES // STRIDE)
    coarse_w = second(np.repeat(c, 2, axis=0), np.repeat(s, 2, axis=0), LANES // (2 * STRIDE))

    shift = np.arange(WINDOW) - WINDOW // 2
    c, s = trig(np.arange(PATCH)[:, None] * shift[None, :])
    c, s = block_diagonal(c, 4), block_diagonal(s, 4)
    inverse = split(np.block([[c, s], [-s, c]]))

    weight = np.where((k == 0) | (k == PATCH // 2), 1.0, 2.0) * keep
    c, s = trig(shift[:, None] * np.arange(KP)[None, :])
    last_high, last_low = split(np.concatenate([c * weight.T, -s * weight.T], axis=1))
    last = np.concatenate([last_high, last_high, last_low], axis=1)
    energy = np.kron(np.eye(4), np.ones((PATCH, WINDOW)))
    return [
        first,
        *fine_w,
        *coarse_w,
        *inverse,
        last,
        np.asarray(energy, np.float32),
        np.asarray(np.broadcast_to(weight, (KP, LANES)), np.float32),
    ]


def split_value(value):
    high = value.astype(BF16)
    return high, (value - high.astype(F32)).astype(BF16)


def matmul(a, b):
    return jnp.dot(a, b, preferred_element_type=F32)


def section_spectra(pixels, first, fine_w, coarse_w, fine_rows, coarse_rows):
    half = matmul(first, jnp.concatenate([pixels, pixels], axis=0))
    width = half.shape[1]
    tiles = width // LANES
    row = lax.broadcasted_iota(jnp.int32, (KP, width), 0)
    fine_in, coarse_in = [], []
    for unit in range(fine_rows + coarse_rows):
        real = half[2 * KP * unit : 2 * KP * unit + KP]
        imag = half[2 * KP * unit + KP : 2 * KP * (unit + 1)]
        sums = real[0:1]
        high = sums.astype(BF16).astype(F32)
        middle = (sums - high).astype(BF16).astype(F32)
        low = sums - high - middle
        real = jnp.where(row == 0, high, real)
        real = jnp.where(row == HALF, middle, real)
        real = jnp.where(row == HALF + 1, low, real)
        target = fine_in if unit < fine_rows else coarse_in
        for tile in range(tiles):
            at = slice(LANES * tile, LANES * (tile + 1))
            target.append(jnp.concatenate([real[:, at], imag[:, at]], axis=1))

    def transform(parts, weights):
        high, low = split_value(jnp.concatenate(parts, axis=0))
        w_high, w_low = weights
        return matmul(high, w_high) + matmul(low, w_high) + matmul(high, w_low)

    fine = transform(fine_in, fine_w)
    coarse = transform(coarse_in, coarse_w)
    wide = 2 * LANES
    lane = lax.broadcasted_iota(jnp.int32, (KP, wide), 1)
    krow = lax.broadcasted_iota(jnp.int32, (KP, wide), 0)
    sign = jnp.where(lane % 2 == 0, 1.0, -1.0).astype(F32)
    dc = (krow == 0) & (lane % PATCH == 0)

    def finish(parts, rows):
        count = len(parts) // rows
        rolled = [pltpu.roll(part, wide - PATCH, 1) for part in parts]
        done = []
        for index, part in enumerate(parts):
            if index % count == count - 1:
                following = jnp.where(lane < wide - PATCH, rolled[index], 0.0)
            else:
                following = jnp.where(lane < wide - PATCH, rolled[index], rolled[index + 1])
            value = part + sign * following
            value = jnp.where(krow == 0, value + value[HALF : HALF + 1] + value[HALF + 1 : HALF + 2], value)
            value = jnp.where(dc, 0.0, value)
            done.append(value)
        return done

    def groups(offset):
        fine_parts = [
            fine[KP * g : KP * (g + 1), offset * wide : (offset + 1) * wide]
            for g in range(fine_rows * tiles)
        ]
        coarse_parts = [
            jnp.concatenate(
                [
                    coarse[KP * g : KP * (g + 1), offset * LANES : (offset + 1) * LANES],
                    coarse[KP * (g + 1) : KP * (g + 2), offset * LANES : (offset + 1) * LANES],
                ],
                axis=1,
            )
            for g in range(0, coarse_rows * tiles, 2)
        ]
        return finish(fine_parts, fine_rows) + finish(coarse_parts, coarse_rows)

    return groups(0), groups(1)


def block_transpose(value):
    row = lax.broadcasted_iota(jnp.int32, value.shape, 0) % 4
    block = lax.broadcasted_iota(jnp.int32, value.shape, 1) // WINDOW
    rows = value.shape[0]
    moved = pltpu.roll(value, 2 * WINDOW, 1)
    other = jnp.where(row < 2, pltpu.roll(moved, rows - 2, 0), pltpu.roll(moved, 2, 0))
    value = jnp.where((row // 2) == (block // 2), value, other)
    right = pltpu.roll(pltpu.roll(value, WINDOW, 1), rows - 1, 0)
    left = pltpu.roll(pltpu.roll(value, LANES - WINDOW, 1), 1, 0)
    other = jnp.where(row % 2 == 0, right, left)
    return jnp.where((row % 2) == (block % 2), value, other)


def compute(const_count, *refs):
    pixels_ref, fine_mask_ref, coarse_mask_ref = refs[:3]
    sources = refs[3 : 3 + const_count]
    fine_out_ref, coarse_out_ref = refs[3 + const_count : 5 + const_count]
    own_ref, near_ref, far_ref, rim_ref, real_ref, imag_ref, sums_ref = refs[5 + const_count : 12 + const_count]
    held = refs[12 + const_count : 12 + 2 * const_count]
    own_sem, const_sem, send_sem, recv_sem = refs[12 + 2 * const_count :]
    sec, strip = lax.axis_index("sec"), lax.axis_index("strip")
    secs, strips = lax.axis_size("sec"), lax.axis_size("strip")

    own_copy = pltpu.make_async_copy(pixels_ref.at[0], own_ref, own_sem)
    own_copy.start()
    const_copies = [
        pltpu.make_async_copy(source, target, const_sem.at[index])
        for index, (source, target) in enumerate(zip(sources, held))
    ]
    for copy in const_copies:
        copy.start()

    barrier = pltpu.get_barrier_semaphore()

    def greet(condition, device):
        @pl.when(condition)
        def _():
            pl.semaphore_signal(barrier, inc=1, device_id=device, device_id_type=MESH)

    greet(sec + 2 < secs, {"sec": sec + 2})
    greet(sec + 1 < secs, {"sec": sec + 1})
    greet(strip + 1 < strips, {"strip": strip + 1})
    targets = lax.min(sec, 2) + lax.min(strip, 1)

    @pl.when(targets >= 1)
    def _():
        pl.semaphore_wait(barrier, targets)

    def remote(source, target, index, device):
        return pltpu.make_async_remote_copy(
            src_ref=source,
            dst_ref=target,
            send_sem=send_sem.at[index],
            recv_sem=recv_sem.at[index],
            device_id=device,
            device_id_type=MESH,
        )

    far_copy = remote(pixels_ref.at[0], far_ref, 0, {"sec": sec - 2})
    near_copy = remote(pixels_ref.at[0], near_ref, 1, {"sec": sec - 1})
    rim_copies = [
        remote(source, rim_ref.at[index], 2 + index, {"strip": strip - 1})
        for index, source in enumerate((pixels_ref.at[0], near_ref, far_ref))
    ]
    up = strip >= 1
    below = strip + 1 < strips
    pl.when(sec >= 2)(far_copy.start)
    pl.when(sec >= 1)(near_copy.start)
    pl.when(up)(rim_copies[0].start)

    def fill(condition, ref, *index):
        @pl.when(condition)
        def _():
            ref[index if index else ...] = jnp.zeros(ref.shape[len(index) :], ref.dtype)

    for d in range(3):
        fill(jnp.logical_not(below & (sec + d < secs)), rim_ref, d)
    fill(sec + 1 >= secs, near_ref)
    fill(sec + 2 >= secs, far_ref)
    sums_ref[...] = jnp.zeros_like(sums_ref)

    fine_rows, fine_cols = fine_mask_ref.shape[1:]
    coarse_rows, coarse_cols = coarse_mask_ref.shape[1:]
    count = (fine_rows * fine_cols + coarse_rows * coarse_cols) // 4
    fine_groups = fine_rows * fine_cols // 4
    (
        first_ref,
        fine_high_ref,
        fine_low_ref,
        coarse_high_ref,
        coarse_low_ref,
        inverse_high_ref,
        inverse_low_ref,
        last_ref,
        energy_ref,
        weight_ref,
    ) = held

    def spread(mask, cols):
        source = lax.broadcasted_iota(jnp.int32, (cols, cols * WINDOW), 0)
        target = lax.broadcasted_iota(jnp.int32, (cols, cols * WINDOW), 1) // WINDOW
        picks = jnp.where(source == target, 1.0, 0.0).astype(BF16)
        return matmul(mask.astype(F32).astype(BF16), picks)

    fine_mask = spread(fine_mask_ref[0], fine_cols)
    coarse_mask = spread(coarse_mask_ref[0], coarse_cols)
    masks = [
        m[r : r + 1, LANES * t : LANES * (t + 1)]
        for m in (fine_mask, coarse_mask)
        for r in range(m.shape[0])
        for t in range(m.shape[1] // LANES)
    ]
    scales = []

    def analyse(section, main_ref):
        pl.when(below & (sec + section < secs))(rim_copies[section].wait_recv)
        weight = jnp.concatenate([weight_ref[...]] * 2, axis=1)
        real, imag = section_spectra(
            jnp.concatenate([main_ref[...], rim_ref[section]], axis=0),
            first_ref[...],
            (fine_high_ref[...], fine_low_ref[...]),
            (coarse_high_ref[...], coarse_low_ref[...]),
            fine_rows,
            coarse_rows,
        )
        for g in range(count):
            real_ref[section, KP * g : KP * (g + 1)] = real[g]
            imag_ref[section, KP * g : KP * (g + 1)] = imag[g]
            power = weight * (real[g] * real[g] + imag[g] * imag[g])
            sums_ref[section, g : g + 1] = jnp.sum(power, axis=0, keepdims=True)
        total = jnp.dot(
            sums_ref[section], energy_ref[...], preferred_element_type=F32, precision=lax.Precision.HIGHEST
        )
        scales.append(1.0 / jnp.sqrt(total * (1.0 / float(PATCH) ** 4) + 1e-05))

    def correlate(d):
        cross_real = real_ref[0] * real_ref[d] + imag_ref[0] * imag_ref[d]
        cross_imag = real_ref[0] * imag_ref[d] - imag_ref[0] * real_ref[d]
        cross = jnp.concatenate([cross_real.astype(BF16), cross_imag.astype(BF16)], axis=1)
        rows = matmul(cross, inverse_high_ref[...]) + matmul(cross, inverse_low_ref[...])
        stacked = []
        for g in range(count):
            part = rows[KP * g : KP * (g + 1)]
            stacked.append(jnp.concatenate([part[:, :LANES], part[:, LANES:]], axis=0))
        high, low = split_value(jnp.concatenate(stacked, axis=1))
        maps = matmul(last_ref[...], jnp.concatenate([high, low, high], axis=0))
        for g in range(count):
            scale = scales[0][g : g + 1] * scales[d][g : g + 1] * masks[g] * (1.0 / float(PATCH) ** 3)
            value = block_transpose(maps[:, LANES * g : LANES * (g + 1)] * scale)
            if g < fine_groups:
                ref, local_g, cols = fine_out_ref, g, fine_cols
            else:
                ref, local_g, cols = coarse_out_ref, g - fine_groups, coarse_cols
            i, j = divmod(4 * local_g, cols)
            for q in range(WINDOW // 4):
                ref[0, d - 1, i, j : j + 4, LANES * q : LANES * (q + 1)] = value[4 * q : 4 * (q + 1)]

    own_copy.wait()
    for copy in const_copies:
        copy.wait()
    has_near, has_far = sec + 1 < secs, sec + 2 < secs
    pl.when(has_near)(near_copy.wait_recv)
    pl.when(has_near & up)(rim_copies[1].start)
    analyse(0, own_ref)
    pl.when(has_far)(far_copy.wait_recv)
    pl.when(has_far & up)(rim_copies[2].start)
    analyse(1, near_ref)
    correlate(1)
    analyse(2, far_ref)
    correlate(2)
    pl.when(sec >= 2)(far_copy.wait_send)
    pl.when(sec >= 1)(near_copy.wait_send)
    pl.when(up)(rim_copies[0].wait_send)
    pl.when(has_near & up)(rim_copies[1].wait_send)
    pl.when(has_far & up)(rim_copies[2].wait_send)


def local(sections, mask_fine, mask_coarse):
    strip_rows, width = sections.shape[1:]
    consts = [jnp.asarray(t) for t in tables(strip_rows)]
    fine_rows, fine_cols = mask_fine.shape[1:]
    coarse_rows, coarse_cols = mask_coarse.shape[1:]
    count = (fine_rows * fine_cols + coarse_rows * coarse_cols) // 4
    vmem = pl.BlockSpec(memory_space=pltpu.VMEM)
    anywhere = pl.BlockSpec(memory_space=pl.ANY)
    flat = WINDOW * WINDOW
    return pl.pallas_call(
        functools.partial(compute, len(consts)),
        out_shape=(
            jax.ShapeDtypeStruct((1, 2, fine_rows, fine_cols, flat), F32),
            jax.ShapeDtypeStruct((1, 2, coarse_rows, coarse_cols, flat), F32),
        ),
        in_specs=[anywhere, vmem, vmem] + [anywhere] * len(consts),
        out_specs=(vmem, vmem),
        scratch_shapes=[
            pltpu.VMEM((strip_rows, width), BF16),
            pltpu.VMEM((strip_rows, width), BF16),
            pltpu.VMEM((strip_rows, width), BF16),
            pltpu.VMEM((3, strip_rows, width), BF16),
            pltpu.VMEM((3, KP * count, 2 * LANES), F32),
            pltpu.VMEM((3, KP * count, 2 * LANES), F32),
            pltpu.VMEM((3, -(-count // 8) * 8, 2 * LANES), F32),
            *[pltpu.VMEM(c.shape, c.dtype) for c in consts],
            pltpu.SemaphoreType.DMA,
            pltpu.SemaphoreType.DMA((len(consts),)),
            pltpu.SemaphoreType.DMA((5,)),
            pltpu.SemaphoreType.DMA((5,)),
        ],
        compiler_params=pltpu.CompilerParams(collective_id=0, has_side_effects=True),
    )(sections, mask_fine, mask_coarse, *consts)


def solution(mesh):
    in_specs = (
        P("sec", "strip", "groups"),
        P("sec", "strip", "groups"),
        P("sec", "strip", "groups"),
    )
    out_specs = (P("sec", None, "strip", "groups", None), P("sec", None, "strip", "groups", None))
    return jax.shard_map(local, mesh=mesh, in_specs=in_specs, out_specs=out_specs, check_vma=False)
```

```python
import functools

import jax
import jax.numpy as jnp
import numpy as np
from jax import lax
from jax.experimental import pallas as pl
from jax.experimental.pallas import tpu as pltpu
from jax.sharding import PartitionSpec as P

PATCH = 64
STRIDE = 32
WINDOW = 32
HALF = PATCH // 2 + 1
KP = 40
CHUNKS = 2
LANES = 128
F32 = jnp.float32
BF16 = jnp.bfloat16
MESH = pl.DeviceIdType.MESH


def trig(phase):
    angle = 2.0 * np.pi / PATCH * np.mod(phase, PATCH)
    return np.round(np.cos(angle), 12), np.round(np.sin(angle), 12)


def split(table):
    high = np.asarray(table, np.float32).astype(BF16)
    low = (np.asarray(table, np.float64) - high.astype(np.float64)).astype(np.float32).astype(BF16)
    return high, low


def block_diagonal(block, count):
    return np.kron(np.eye(count), block)


def tables(strip_rows):
    fine_rows = strip_rows // STRIDE
    coarse_rows = strip_rows // (2 * STRIDE)
    height = strip_rows + PATCH
    k = np.arange(KP)[:, None]
    keep = (k < HALF).astype(np.float64)
    x = np.arange(height)[None, :]
    units = []
    for i in range(fine_rows):
        c, s = trig(k * (x - STRIDE * i))
        inside = ((x >= STRIDE * i) & (x < STRIDE * i + PATCH)) * keep
        units += [c * inside, -s * inside]
    for i in range(coarse_rows):
        xc = x // 2 - STRIDE * i
        c, s = trig(k * xc)
        inside = ((xc >= 0) & (xc < PATCH)) * keep * 0.25
        units += [c * inside, -s * inside]
    a_high, a_low = split(np.concatenate(units, axis=0))
    first = np.concatenate([a_high, a_low], axis=1)

    freq = np.arange(PATCH)[None, :]
    y = np.arange(STRIDE)[:, None]
    c, s = trig(y * freq)

    def second(c, s, count):
        c, s = block_diagonal(c, count), block_diagonal(s, count)
        return split(np.block([[c, -s], [s, c]]))

    fine_w = second(c, s, LANES // STRIDE)
    coarse_w = second(np.repeat(c, 2, axis=0), np.repeat(s, 2, axis=0), LANES // (2 * STRIDE))

    shift = np.arange(WINDOW) - WINDOW // 2
    c, s = trig(np.arange(PATCH)[:, None] * shift[None, :])
    c, s = block_diagonal(c, 4), block_diagonal(s, 4)
    inverse = split(np.block([[c, s], [-s, c]]))

    weight = np.where((k == 0) | (k == PATCH // 2), 1.0, 2.0) * keep
    c, s = trig(shift[:, None] * np.arange(KP)[None, :])
    last_high, last_low = split(np.concatenate([c * weight.T, -s * weight.T], axis=1))
    last = np.concatenate([last_high, last_high, last_low], axis=1)
    energy = np.kron(np.eye(4), np.ones((PATCH, WINDOW)))
    return [
        first,
        *fine_w,
        *coarse_w,
        *inverse,
        last,
        np.asarray(energy, np.float32),
        np.asarray(np.broadcast_to(weight, (KP, LANES)), np.float32),
    ]


def split_value(value):
    high = value.astype(BF16)
    return high, (value - high.astype(F32)).astype(BF16)


def matmul(a, b):
    return jnp.dot(a, b, preferred_element_type=F32)


def section_spectra(pixels, first, fine_w, coarse_w, fine_rows, coarse_rows):
    half = matmul(first, jnp.concatenate([pixels, pixels], axis=0))
    width = half.shape[1]
    tiles = width // LANES
    row = lax.broadcasted_iota(jnp.int32, (KP, width), 0)
    fine_in, coarse_in = [], []
    for unit in range(fine_rows + coarse_rows):
        real = half[2 * KP * unit : 2 * KP * unit + KP]
        imag = half[2 * KP * unit + KP : 2 * KP * (unit + 1)]
        sums = real[0:1]
        high = sums.astype(BF16).astype(F32)
        middle = (sums - high).astype(BF16).astype(F32)
        low = sums - high - middle
        real = jnp.where(row == 0, high, real)
        real = jnp.where(row == HALF, middle, real)
        real = jnp.where(row == HALF + 1, low, real)
        target = fine_in if unit < fine_rows else coarse_in
        for tile in range(tiles):
            at = slice(LANES * tile, LANES * (tile + 1))
            target.append(jnp.concatenate([real[:, at], imag[:, at]], axis=1))

    def transform(parts, weights):
        high, low = split_value(jnp.concatenate(parts, axis=0))
        w_high, w_low = weights
        return matmul(high, w_high) + matmul(low, w_high) + matmul(high, w_low)

    fine = transform(fine_in, fine_w)
    coarse = transform(coarse_in, coarse_w)
    wide = 2 * LANES
    lane = lax.broadcasted_iota(jnp.int32, (KP, wide), 1)
    krow = lax.broadcasted_iota(jnp.int32, (KP, wide), 0)
    sign = jnp.where(lane % 2 == 0, 1.0, -1.0).astype(F32)
    dc = (krow == 0) & (lane % PATCH == 0)

    def finish(parts, rows):
        count = len(parts) // rows
        rolled = [pltpu.roll(part, wide - PATCH, 1) for part in parts]
        done = []
        for index, part in enumerate(parts):
            if index % count == count - 1:
                following = jnp.where(lane < wide - PATCH, rolled[index], 0.0)
            else:
                following = jnp.where(lane < wide - PATCH, rolled[index], rolled[index + 1])
            value = part + sign * following
            value = jnp.where(krow == 0, value + value[HALF : HALF + 1] + value[HALF + 1 : HALF + 2], value)
            value = jnp.where(dc, 0.0, value)
            done.append(value)
        return done

    def groups(offset):
        fine_parts = [
            fine[KP * g : KP * (g + 1), offset * wide : (offset + 1) * wide]
            for g in range(fine_rows * tiles)
        ]
        coarse_parts = [
            jnp.concatenate(
                [
                    coarse[KP * g : KP * (g + 1), offset * LANES : (offset + 1) * LANES],
                    coarse[KP * (g + 1) : KP * (g + 2), offset * LANES : (offset + 1) * LANES],
                ],
                axis=1,
            )
            for g in range(0, coarse_rows * tiles, 2)
        ]
        return finish(fine_parts, fine_rows) + finish(coarse_parts, coarse_rows)

    return groups(0), groups(1)


def block_transpose(value):
    row = lax.broadcasted_iota(jnp.int32, value.shape, 0) % 4
    block = lax.broadcasted_iota(jnp.int32, value.shape, 1) // WINDOW
    rows = value.shape[0]
    moved = pltpu.roll(value, 2 * WINDOW, 1)
    other = jnp.where(row < 2, pltpu.roll(moved, rows - 2, 0), pltpu.roll(moved, 2, 0))
    value = jnp.where((row // 2) == (block // 2), value, other)
    right = pltpu.roll(pltpu.roll(value, WINDOW, 1), rows - 1, 0)
    left = pltpu.roll(pltpu.roll(value, LANES - WINDOW, 1), 1, 0)
    other = jnp.where(row % 2 == 0, right, left)
    return jnp.where((row % 2) == (block % 2), value, other)


def compute(const_count, *refs):
    pixels_ref, fine_mask_ref, coarse_mask_ref = refs[:3]
    sources = refs[3 : 3 + const_count]
    maps_ref = refs[3 + const_count]
    own_ref, near_ref, far_ref, rim_ref, real_ref, imag_ref, sums_ref = refs[4 + const_count : 11 + const_count]
    held = refs[11 + const_count : 11 + 2 * const_count]
    own_sem, const_sem, send_sem, recv_sem = refs[11 + 2 * const_count :]
    sec, strip = lax.axis_index("sec"), lax.axis_index("strip")
    secs, strips = lax.axis_size("sec"), lax.axis_size("strip")

    own_copy = pltpu.make_async_copy(pixels_ref.at[0], own_ref, own_sem)
    own_copy.start()
    const_copies = [
        pltpu.make_async_copy(source, target, const_sem.at[index])
        for index, (source, target) in enumerate(zip(sources, held))
    ]
    for copy in const_copies:
        copy.start()

    barrier = pltpu.get_barrier_semaphore()

    def greet(condition, device):
        @pl.when(condition)
        def _():
            pl.semaphore_signal(barrier, inc=1, device_id=device, device_id_type=MESH)

    greet(sec + 1 < secs, {"sec": sec + 1})
    greet(strip + 1 < strips, {"strip": strip + 1})
    targets = lax.min(sec, 1) + lax.min(strip, 1)

    @pl.when(targets >= 1)
    def _():
        pl.semaphore_wait(barrier, targets)

    piece = pixels_ref.shape[1] // CHUNKS

    def remote(source, target, flow, chunk, device):
        rows = pl.ds(piece * chunk, piece)
        return pltpu.make_async_remote_copy(
            src_ref=source.at[rows],
            dst_ref=target.at[rows],
            send_sem=send_sem.at[flow, chunk],
            recv_sem=recv_sem.at[flow, chunk],
            device_id=device,
            device_id_type=MESH,
        )

    above, before = {"strip": strip - 1}, {"sec": sec - 1}
    rim_copies = [
        [remote(source, rim_ref.at[index], index, c, above) for c in range(CHUNKS)]
        for index, source in enumerate((pixels_ref.at[0], near_ref, far_ref))
    ]
    near_copies = [remote(pixels_ref.at[0], near_ref, 3, c, before) for c in range(CHUNKS)]
    far_copies = [remote(near_ref, far_ref, 4, c, before) for c in range(CHUNKS)]
    up = strip >= 1
    below = strip + 1 < strips
    has_near, has_far = sec + 1 < secs, sec + 2 < secs

    def each(condition, copies, method):
        @pl.when(condition)
        def _():
            for copy in copies:
                getattr(copy, method)()

    each(sec >= 1, near_copies, "start")
    each(up, rim_copies[0], "start")

    def fill(condition, ref, *index):
        @pl.when(condition)
        def _():
            ref[index if index else ...] = jnp.zeros(ref.shape[len(index) :], ref.dtype)

    for d in range(3):
        fill(jnp.logical_not(below & (sec + d < secs)), rim_ref, d)
    fill(sec + 1 >= secs, near_ref)
    fill(sec + 2 >= secs, far_ref)
    sums_ref[...] = jnp.zeros_like(sums_ref)

    fine_rows, fine_cols = fine_mask_ref.shape[1:]
    coarse_rows, coarse_cols = coarse_mask_ref.shape[1:]
    count = (fine_rows * fine_cols + coarse_rows * coarse_cols) // 4
    (
        first_ref,
        fine_high_ref,
        fine_low_ref,
        coarse_high_ref,
        coarse_low_ref,
        inverse_high_ref,
        inverse_low_ref,
        last_ref,
        energy_ref,
        weight_ref,
    ) = held

    def spread(mask, cols):
        source = lax.broadcasted_iota(jnp.int32, (cols, cols * WINDOW), 0)
        target = lax.broadcasted_iota(jnp.int32, (cols, cols * WINDOW), 1) // WINDOW
        picks = jnp.where(source == target, 1.0, 0.0).astype(BF16)
        return matmul(mask.astype(F32).astype(BF16), picks)

    fine_mask = spread(fine_mask_ref[0], fine_cols)
    coarse_mask = spread(coarse_mask_ref[0], coarse_cols)
    masks = [
        m[r : r + 1, LANES * t : LANES * (t + 1)]
        for m in (fine_mask, coarse_mask)
        for r in range(m.shape[0])
        for t in range(m.shape[1] // LANES)
    ]
    scales = []

    def analyse(section, main_ref):
        each(below & (sec + section < secs), rim_copies[section], "wait_recv")
        weight = jnp.concatenate([weight_ref[...]] * 2, axis=1)
        real, imag = section_spectra(
            jnp.concatenate([main_ref[...], rim_ref[section]], axis=0),
            first_ref[...],
            (fine_high_ref[...], fine_low_ref[...]),
            (coarse_high_ref[...], coarse_low_ref[...]),
            fine_rows,
            coarse_rows,
        )
        for g in range(count):
            real_ref[section, KP * g : KP * (g + 1)] = real[g]
            imag_ref[section, KP * g : KP * (g + 1)] = imag[g]
            power = weight * (real[g] * real[g] + imag[g] * imag[g])
            sums_ref[section, g : g + 1] = jnp.sum(power, axis=0, keepdims=True)
        total = jnp.dot(
            sums_ref[section], energy_ref[...], preferred_element_type=F32, precision=lax.Precision.HIGHEST
        )
        scales.append(1.0 / jnp.sqrt(total * (1.0 / float(PATCH) ** 4) + 1e-05))

    def correlate(d):
        cross_real = real_ref[0] * real_ref[d] + imag_ref[0] * imag_ref[d]
        cross_imag = real_ref[0] * imag_ref[d] - imag_ref[0] * real_ref[d]
        cross = jnp.concatenate([cross_real.astype(BF16), cross_imag.astype(BF16)], axis=1)
        rows = matmul(cross, inverse_high_ref[...]) + matmul(cross, inverse_low_ref[...])
        stacked = []
        for g in range(count):
            part = rows[KP * g : KP * (g + 1)]
            stacked.append(jnp.concatenate([part[:, :LANES], part[:, LANES:]], axis=0))
        high, low = split_value(jnp.concatenate(stacked, axis=1))
        maps = matmul(last_ref[...], jnp.concatenate([high, low, high], axis=0))
        for g in range(count):
            scale = scales[0][g : g + 1] * scales[d][g : g + 1] * masks[g] * (1.0 / float(PATCH) ** 3)
            maps_ref[d - 1, g] = maps[:, LANES * g : LANES * (g + 1)] * scale

    @pl.when(has_near)
    def _():
        for c in range(CHUNKS):
            near_copies[c].wait_recv()
            pl.when(sec >= 1)(far_copies[c].start)
            pl.when(up)(rim_copies[1][c].start)

    own_copy.wait()
    for copy in const_copies:
        copy.wait()
    analyse(0, own_ref)

    @pl.when(has_far)
    def _():
        for c in range(CHUNKS):
            far_copies[c].wait_recv()
            pl.when(up)(rim_copies[2][c].start)

    analyse(1, near_ref)
    correlate(1)
    analyse(2, far_ref)
    correlate(2)
    each(sec >= 1, near_copies, "wait_send")
    each(has_near & (sec >= 1), far_copies, "wait_send")
    each(up, rim_copies[0], "wait_send")
    each(has_near & up, rim_copies[1], "wait_send")
    each(has_far & up, rim_copies[2], "wait_send")


def arrange(maps_ref, fine_out_ref, coarse_out_ref):
    fine_rows, fine_cols = fine_out_ref.shape[2:4]
    coarse_rows, coarse_cols = coarse_out_ref.shape[2:4]
    fine_groups = fine_rows * fine_cols // 4
    count = fine_groups + coarse_rows * coarse_cols // 4
    for d in range(2):
        for g in range(count):
            value = block_transpose(maps_ref[d, g])
            if g < fine_groups:
                ref, local_g, cols = fine_out_ref, g, fine_cols
            else:
                ref, local_g, cols = coarse_out_ref, g - fine_groups, coarse_cols
            i, j = divmod(4 * local_g, cols)
            for q in range(WINDOW // 4):
                ref[0, d, i, j : j + 4, LANES * q : LANES * (q + 1)] = value[4 * q : 4 * (q + 1)]


def local(sections, mask_fine, mask_coarse):
    strip_rows, width = sections.shape[1:]
    consts = [jnp.asarray(t) for t in tables(strip_rows)]
    fine_rows, fine_cols = mask_fine.shape[1:]
    coarse_rows, coarse_cols = mask_coarse.shape[1:]
    count = (fine_rows * fine_cols + coarse_rows * coarse_cols) // 4
    vmem = pl.BlockSpec(memory_space=pltpu.VMEM)
    anywhere = pl.BlockSpec(memory_space=pl.ANY)
    flat = WINDOW * WINDOW
    maps = pl.pallas_call(
        functools.partial(compute, len(consts)),
        out_shape=jax.ShapeDtypeStruct((2, count, WINDOW, LANES), F32),
        in_specs=[anywhere, vmem, vmem] + [anywhere] * len(consts),
        out_specs=vmem,
        scratch_shapes=[
            pltpu.VMEM((strip_rows, width), BF16),
            pltpu.VMEM((strip_rows, width), BF16),
            pltpu.VMEM((strip_rows, width), BF16),
            pltpu.VMEM((3, strip_rows, width), BF16),
            pltpu.VMEM((3, KP * count, 2 * LANES), F32),
            pltpu.VMEM((3, KP * count, 2 * LANES), F32),
            pltpu.VMEM((3, -(-count // 8) * 8, 2 * LANES), F32),
            *[pltpu.VMEM(c.shape, c.dtype) for c in consts],
            pltpu.SemaphoreType.DMA,
            pltpu.SemaphoreType.DMA((len(consts),)),
            pltpu.SemaphoreType.DMA((5, CHUNKS)),
            pltpu.SemaphoreType.DMA((5, CHUNKS)),
        ],
        compiler_params=pltpu.CompilerParams(collective_id=0, has_side_effects=True),
    )(sections, mask_fine, mask_coarse, *consts)
    return pl.pallas_call(
        arrange,
        out_shape=(
            jax.ShapeDtypeStruct((1, 2, fine_rows, fine_cols, flat), F32),
            jax.ShapeDtypeStruct((1, 2, coarse_rows, coarse_cols, flat), F32),
        ),
        in_specs=[vmem],
        out_specs=(vmem, vmem),
    )(maps)


def solution(mesh):
    in_specs = (
        P("sec", "strip", "groups"),
        P("sec", "strip", "groups"),
        P("sec", "strip", "groups"),
    )
    out_specs = (P("sec", None, "strip", "groups", None), P("sec", None, "strip", "groups", None))
    return jax.shard_map(local, mesh=mesh, in_specs=in_specs, out_specs=out_specs, check_vma=False)
```

```python
import functools

import jax
import jax.numpy as jnp
import numpy as np
from jax import lax
from jax.experimental import pallas as pl
from jax.experimental.pallas import tpu as pltpu
from jax.sharding import PartitionSpec as P

PATCH = 64
STRIDE = 32
WINDOW = 32
HALF = PATCH // 2 + 1
KP = 40
CHUNKS = 4
LANES = 128
F32 = jnp.float32
BF16 = jnp.bfloat16
MESH = pl.DeviceIdType.MESH


def trig(phase):
    angle = 2.0 * np.pi / PATCH * np.mod(phase, PATCH)
    return np.round(np.cos(angle), 12), np.round(np.sin(angle), 12)


def split(table):
    high = np.asarray(table, np.float32).astype(BF16)
    low = (np.asarray(table, np.float64) - high.astype(np.float64)).astype(np.float32).astype(BF16)
    return high, low


def block_diagonal(block, count):
    return np.kron(np.eye(count), block)


def tables(strip_rows):
    fine_rows = strip_rows // STRIDE
    coarse_rows = strip_rows // (2 * STRIDE)
    height = strip_rows + PATCH
    k = np.arange(KP)[:, None]
    keep = (k < HALF).astype(np.float64)
    x = np.arange(height)[None, :]
    units = []
    for i in range(fine_rows):
        c, s = trig(k * (x - STRIDE * i))
        inside = ((x >= STRIDE * i) & (x < STRIDE * i + PATCH)) * keep
        units += [c * inside, -s * inside]
    for i in range(coarse_rows):
        xc = x // 2 - STRIDE * i
        c, s = trig(k * xc)
        inside = ((xc >= 0) & (xc < PATCH)) * keep * 0.25
        units += [c * inside, -s * inside]
    a_high, a_low = split(np.concatenate(units, axis=0))
    first = np.concatenate([a_high, a_low], axis=1)

    freq = np.arange(PATCH)[None, :]
    y = np.arange(STRIDE)[:, None]
    c, s = trig(y * freq)

    def second(c, s, count):
        c, s = block_diagonal(c, count), block_diagonal(s, count)
        return split(np.block([[c, -s], [s, c]]))

    fine_w = second(c, s, LANES // STRIDE)
    coarse_w = second(np.repeat(c, 2, axis=0), np.repeat(s, 2, axis=0), LANES // (2 * STRIDE))

    shift = np.arange(WINDOW) - WINDOW // 2
    c, s = trig(np.arange(PATCH)[:, None] * shift[None, :])
    c, s = block_diagonal(c, 4), block_diagonal(s, 4)
    inverse = split(np.block([[c, s], [-s, c]]))

    weight = np.where((k == 0) | (k == PATCH // 2), 1.0, 2.0) * keep
    c, s = trig(shift[:, None] * np.arange(KP)[None, :])
    last_high, last_low = split(np.concatenate([c * weight.T, -s * weight.T], axis=1))
    last = np.concatenate([last_high, last_high, last_low], axis=1)
    energy = np.kron(np.eye(4), np.ones((PATCH, WINDOW)))
    return [
        first,
        *fine_w,
        *coarse_w,
        *inverse,
        last,
        np.asarray(energy, np.float32),
        np.asarray(np.broadcast_to(weight, (KP, LANES)), np.float32),
    ]


def split_value(value):
    high = value.astype(BF16)
    return high, (value - high.astype(F32)).astype(BF16)


def matmul(a, b):
    return jnp.dot(a, b, preferred_element_type=F32)


def section_spectra(pixels, first, fine_w, coarse_w, fine_rows, coarse_rows):
    half = matmul(first, jnp.concatenate([pixels, pixels], axis=0))
    width = half.shape[1]
    tiles = width // LANES
    row = lax.broadcasted_iota(jnp.int32, (KP, width), 0)
    fine_in, coarse_in = [], []
    for unit in range(fine_rows + coarse_rows):
        real = half[2 * KP * unit : 2 * KP * unit + KP]
        imag = half[2 * KP * unit + KP : 2 * KP * (unit + 1)]
        sums = real[0:1]
        high = sums.astype(BF16).astype(F32)
        middle = (sums - high).astype(BF16).astype(F32)
        low = sums - high - middle
        real = jnp.where(row == 0, high, real)
        real = jnp.where(row == HALF, middle, real)
        real = jnp.where(row == HALF + 1, low, real)
        target = fine_in if unit < fine_rows else coarse_in
        for tile in range(tiles):
            at = slice(LANES * tile, LANES * (tile + 1))
            target.append(jnp.concatenate([real[:, at], imag[:, at]], axis=1))

    def transform(parts, weights):
        high, low = split_value(jnp.concatenate(parts, axis=0))
        w_high, w_low = weights
        return matmul(high, w_high) + matmul(low, w_high) + matmul(high, w_low)

    fine = transform(fine_in, fine_w)
    coarse = transform(coarse_in, coarse_w)
    wide = 2 * LANES
    lane = lax.broadcasted_iota(jnp.int32, (KP, wide), 1)
    krow = lax.broadcasted_iota(jnp.int32, (KP, wide), 0)
    sign = jnp.where(lane % 2 == 0, 1.0, -1.0).astype(F32)
    dc = (krow == 0) & (lane % PATCH == 0)

    def finish(parts, rows):
        count = len(parts) // rows
        rolled = [pltpu.roll(part, wide - PATCH, 1) for part in parts]
        done = []
        for index, part in enumerate(parts):
            if index % count == count - 1:
                following = jnp.where(lane < wide - PATCH, rolled[index], 0.0)
            else:
                following = jnp.where(lane < wide - PATCH, rolled[index], rolled[index + 1])
            value = part + sign * following
            value = jnp.where(krow == 0, value + value[HALF : HALF + 1] + value[HALF + 1 : HALF + 2], value)
            value = jnp.where(dc, 0.0, value)
            done.append(value)
        return done

    def groups(offset):
        fine_parts = [
            fine[KP * g : KP * (g + 1), offset * wide : (offset + 1) * wide]
            for g in range(fine_rows * tiles)
        ]
        coarse_parts = [
            jnp.concatenate(
                [
                    coarse[KP * g : KP * (g + 1), offset * LANES : (offset + 1) * LANES],
                    coarse[KP * (g + 1) : KP * (g + 2), offset * LANES : (offset + 1) * LANES],
                ],
                axis=1,
            )
            for g in range(0, coarse_rows * tiles, 2)
        ]
        return finish(fine_parts, fine_rows) + finish(coarse_parts, coarse_rows)

    return groups(0), groups(1)


def block_transpose(value):
    row = lax.broadcasted_iota(jnp.int32, value.shape, 0) % 4
    block = lax.broadcasted_iota(jnp.int32, value.shape, 1) // WINDOW
    rows = value.shape[0]
    moved = pltpu.roll(value, 2 * WINDOW, 1)
    other = jnp.where(row < 2, pltpu.roll(moved, rows - 2, 0), pltpu.roll(moved, 2, 0))
    value = jnp.where((row // 2) == (block // 2), value, other)
    right = pltpu.roll(pltpu.roll(value, WINDOW, 1), rows - 1, 0)
    left = pltpu.roll(pltpu.roll(value, LANES - WINDOW, 1), 1, 0)
    other = jnp.where(row % 2 == 0, right, left)
    return jnp.where((row % 2) == (block % 2), value, other)


def compute(const_count, *refs):
    pixels_ref, fine_mask_ref, coarse_mask_ref = refs[:3]
    sources = refs[3 : 3 + const_count]
    maps_ref = refs[3 + const_count]
    own_ref, near_ref, far_ref, rim_ref, real_ref, imag_ref, sums_ref = refs[4 + const_count : 11 + const_count]
    held = refs[11 + const_count : 11 + 2 * const_count]
    own_sem, const_sem, send_sem, recv_sem = refs[11 + 2 * const_count :]
    sec, strip = lax.axis_index("sec"), lax.axis_index("strip")
    secs, strips = lax.axis_size("sec"), lax.axis_size("strip")

    own_copy = pltpu.make_async_copy(pixels_ref.at[0], own_ref, own_sem)
    own_copy.start()
    const_copies = [
        pltpu.make_async_copy(source, target, const_sem.at[index])
        for index, (source, target) in enumerate(zip(sources, held))
    ]
    for copy in const_copies:
        copy.start()

    barrier = pltpu.get_barrier_semaphore()

    def greet(condition, device):
        @pl.when(condition)
        def _():
            pl.semaphore_signal(barrier, inc=1, device_id=device, device_id_type=MESH)

    greet(sec + 1 < secs, {"sec": sec + 1})
    greet(strip + 1 < strips, {"strip": strip + 1})
    targets = lax.min(sec, 1) + lax.min(strip, 1)

    @pl.when(targets >= 1)
    def _():
        pl.semaphore_wait(barrier, targets)

    piece = pixels_ref.shape[1] // CHUNKS

    def remote(source, target, flow, chunk, device):
        rows = pl.ds(piece * chunk, piece)
        return pltpu.make_async_remote_copy(
            src_ref=source.at[rows],
            dst_ref=target.at[rows],
            send_sem=send_sem.at[flow, chunk],
            recv_sem=recv_sem.at[flow, chunk],
            device_id=device,
            device_id_type=MESH,
        )

    above, before = {"strip": strip - 1}, {"sec": sec - 1}
    rim_copies = [
        [remote(source, rim_ref.at[index], index, c, above) for c in range(CHUNKS)]
        for index, source in enumerate((pixels_ref.at[0], near_ref, far_ref))
    ]
    near_copies = [remote(pixels_ref.at[0], near_ref, 3, c, before) for c in range(CHUNKS)]
    far_copies = [remote(near_ref, far_ref, 4, c, before) for c in range(CHUNKS)]
    up = strip >= 1
    below = strip + 1 < strips
    has_near, has_far = sec + 1 < secs, sec + 2 < secs

    def each(condition, copies, method):
        @pl.when(condition)
        def _():
            for copy in copies:
                getattr(copy, method)()

    for c in range(CHUNKS):
        pl.when(up)(rim_copies[0][c].start)
        pl.when(sec >= 1)(near_copies[c].start)

    def fill(condition, ref, *index):
        @pl.when(condition)
        def _():
            ref[index if index else ...] = jnp.zeros(ref.shape[len(index) :], ref.dtype)

    for d in range(3):
        fill(jnp.logical_not(below & (sec + d < secs)), rim_ref, d)
    fill(sec + 1 >= secs, near_ref)
    fill(sec + 2 >= secs, far_ref)
    sums_ref[...] = jnp.zeros_like(sums_ref)

    fine_rows, fine_cols = fine_mask_ref.shape[1:]
    coarse_rows, coarse_cols = coarse_mask_ref.shape[1:]
    count = (fine_rows * fine_cols + coarse_rows * coarse_cols) // 4
    (
        first_ref,
        fine_high_ref,
        fine_low_ref,
        coarse_high_ref,
        coarse_low_ref,
        inverse_high_ref,
        inverse_low_ref,
        last_ref,
        energy_ref,
        weight_ref,
    ) = held

    def spread(mask, cols):
        source = lax.broadcasted_iota(jnp.int32, (cols, cols * WINDOW), 0)
        target = lax.broadcasted_iota(jnp.int32, (cols, cols * WINDOW), 1) // WINDOW
        picks = jnp.where(source == target, 1.0, 0.0).astype(BF16)
        return matmul(mask.astype(F32).astype(BF16), picks)

    fine_mask = spread(fine_mask_ref[0], fine_cols)
    coarse_mask = spread(coarse_mask_ref[0], coarse_cols)
    masks = [
        m[r : r + 1, LANES * t : LANES * (t + 1)]
        for m in (fine_mask, coarse_mask)
        for r in range(m.shape[0])
        for t in range(m.shape[1] // LANES)
    ]
    scales = []

    def analyse(section, main_ref):
        each(below & (sec + section < secs), rim_copies[section], "wait_recv")
        weight = jnp.concatenate([weight_ref[...]] * 2, axis=1)
        real, imag = section_spectra(
            jnp.concatenate([main_ref[...], rim_ref[section]], axis=0),
            first_ref[...],
            (fine_high_ref[...], fine_low_ref[...]),
            (coarse_high_ref[...], coarse_low_ref[...]),
            fine_rows,
            coarse_rows,
        )
        for g in range(count):
            real_ref[section, KP * g : KP * (g + 1)] = real[g]
            imag_ref[section, KP * g : KP * (g + 1)] = imag[g]
            power = weight * (real[g] * real[g] + imag[g] * imag[g])
            sums_ref[section, g : g + 1] = jnp.sum(power, axis=0, keepdims=True)
        total = jnp.dot(
            sums_ref[section], energy_ref[...], preferred_element_type=F32, precision=lax.Precision.HIGHEST
        )
        scales.append(1.0 / jnp.sqrt(total * (1.0 / float(PATCH) ** 4) + 1e-05))

    def correlate(d):
        cross_real = real_ref[0] * real_ref[d] + imag_ref[0] * imag_ref[d]
        cross_imag = real_ref[0] * imag_ref[d] - imag_ref[0] * real_ref[d]
        cross = jnp.concatenate([cross_real.astype(BF16), cross_imag.astype(BF16)], axis=1)
        rows = matmul(cross, inverse_high_ref[...]) + matmul(cross, inverse_low_ref[...])
        stacked = []
        for g in range(count):
            part = rows[KP * g : KP * (g + 1)]
            stacked.append(jnp.concatenate([part[:, :LANES], part[:, LANES:]], axis=0))
        high, low = split_value(jnp.concatenate(stacked, axis=1))
        maps = matmul(last_ref[...], jnp.concatenate([high, low, high], axis=0))
        for g in range(count):
            scale = scales[0][g : g + 1] * scales[d][g : g + 1] * masks[g] * (1.0 / float(PATCH) ** 3)
            maps_ref[d - 1, g] = maps[:, LANES * g : LANES * (g + 1)] * scale

    @pl.when(has_near)
    def _():
        for c in range(CHUNKS):
            near_copies[c].wait_recv()
            pl.when(up)(rim_copies[1][c].start)
            pl.when(sec >= 1)(far_copies[c].start)

    own_copy.wait()
    for copy in const_copies:
        copy.wait()
    analyse(0, own_ref)

    @pl.when(has_far)
    def _():
        for c in range(CHUNKS):
            far_copies[c].wait_recv()
            pl.when(up)(rim_copies[2][c].start)

    analyse(1, near_ref)
    correlate(1)
    analyse(2, far_ref)
    correlate(2)
    each(sec >= 1, near_copies, "wait_send")
    each(has_near & (sec >= 1), far_copies, "wait_send")
    each(up, rim_copies[0], "wait_send")
    each(has_near & up, rim_copies[1], "wait_send")
    each(has_far & up, rim_copies[2], "wait_send")


def arrange(maps_ref, fine_out_ref, coarse_out_ref):
    fine_rows, fine_cols = fine_out_ref.shape[2:4]
    coarse_rows, coarse_cols = coarse_out_ref.shape[2:4]
    fine_groups = fine_rows * fine_cols // 4
    count = fine_groups + coarse_rows * coarse_cols // 4
    for d in range(1):
        for g in range(count):
            value = block_transpose(maps_ref[d, g])
            if g < fine_groups:
                ref, local_g, cols = fine_out_ref, g, fine_cols
            else:
                ref, local_g, cols = coarse_out_ref, g - fine_groups, coarse_cols
            i, j = divmod(4 * local_g, cols)
            for q in range(WINDOW // 4):
                ref[0, d, i, j : j + 4, LANES * q : LANES * (q + 1)] = value[4 * q : 4 * (q + 1)]


def local(sections, mask_fine, mask_coarse):
    strip_rows, width = sections.shape[1:]
    consts = [jnp.asarray(t) for t in tables(strip_rows)]
    fine_rows, fine_cols = mask_fine.shape[1:]
    coarse_rows, coarse_cols = mask_coarse.shape[1:]
    count = (fine_rows * fine_cols + coarse_rows * coarse_cols) // 4
    vmem = pl.BlockSpec(memory_space=pltpu.VMEM)
    anywhere = pl.BlockSpec(memory_space=pl.ANY)
    flat = WINDOW * WINDOW
    maps = pl.pallas_call(
        functools.partial(compute, len(consts)),
        out_shape=jax.ShapeDtypeStruct((2, count, WINDOW, LANES), F32),
        in_specs=[anywhere, vmem, vmem] + [anywhere] * len(consts),
        out_specs=vmem,
        scratch_shapes=[
            pltpu.VMEM((strip_rows, width), BF16),
            pltpu.VMEM((strip_rows, width), BF16),
            pltpu.VMEM((strip_rows, width), BF16),
            pltpu.VMEM((3, strip_rows, width), BF16),
            pltpu.VMEM((3, KP * count, 2 * LANES), F32),
            pltpu.VMEM((3, KP * count, 2 * LANES), F32),
            pltpu.VMEM((3, -(-count // 8) * 8, 2 * LANES), F32),
            *[pltpu.VMEM(c.shape, c.dtype) for c in consts],
            pltpu.SemaphoreType.DMA,
            pltpu.SemaphoreType.DMA((len(consts),)),
            pltpu.SemaphoreType.DMA((5, CHUNKS)),
            pltpu.SemaphoreType.DMA((5, CHUNKS)),
        ],
        compiler_params=pltpu.CompilerParams(collective_id=0, has_side_effects=True),
    )(sections, mask_fine, mask_coarse, *consts)
    return pl.pallas_call(
        arrange,
        out_shape=(
            jax.ShapeDtypeStruct((1, 2, fine_rows, fine_cols, flat), F32),
            jax.ShapeDtypeStruct((1, 2, coarse_rows, coarse_cols, flat), F32),
        ),
        grid=(2,),
        in_specs=[pl.BlockSpec((1, count, WINDOW, LANES), lambda d: (d, 0, 0, 0))],
        out_specs=(
            pl.BlockSpec((1, 1, fine_rows, fine_cols, flat), lambda d: (0, d, 0, 0, 0)),
            pl.BlockSpec((1, 1, coarse_rows, coarse_cols, flat), lambda d: (0, d, 0, 0, 0)),
        ),
    )(maps)


def solution(mesh):
    in_specs = (
        P("sec", "strip", "groups"),
        P("sec", "strip", "groups"),
        P("sec", "strip", "groups"),
    )
    out_specs = (P("sec", None, "strip", "groups", None), P("sec", None, "strip", "groups", None))
    return jax.shard_map(local, mesh=mesh, in_specs=in_specs, out_specs=out_specs, check_vma=False)
```

```python
import functools

import jax
import jax.numpy as jnp
import numpy as np
from jax import lax
from jax.experimental import pallas as pl
from jax.experimental.pallas import tpu as pltpu
from jax.sharding import PartitionSpec as P

PATCH = 64
STRIDE = 32
WINDOW = 32
HALF = PATCH // 2 + 1
KP = 40
CHUNKS = 4
LANES = 128
F32 = jnp.float32
BF16 = jnp.bfloat16
MESH = pl.DeviceIdType.MESH


def trig(phase):
    angle = 2.0 * np.pi / PATCH * np.mod(phase, PATCH)
    return np.round(np.cos(angle), 12), np.round(np.sin(angle), 12)


def split(table):
    high = np.asarray(table, np.float32).astype(BF16)
    low = (np.asarray(table, np.float64) - high.astype(np.float64)).astype(np.float32).astype(BF16)
    return high, low


def block_diagonal(block, count):
    return np.kron(np.eye(count), block)


def tables(strip_rows):
    fine_rows = strip_rows // STRIDE
    coarse_rows = strip_rows // (2 * STRIDE)
    height = strip_rows + PATCH
    k = np.arange(KP)[:, None]
    keep = (k < HALF).astype(np.float64)
    x = np.arange(height)[None, :]
    units = []
    for i in range(fine_rows):
        c, s = trig(k * (x - STRIDE * i))
        inside = ((x >= STRIDE * i) & (x < STRIDE * i + PATCH)) * keep
        units += [c * inside, -s * inside]
    for i in range(coarse_rows):
        xc = x // 2 - STRIDE * i
        c, s = trig(k * xc)
        inside = ((xc >= 0) & (xc < PATCH)) * keep * 0.25
        units += [c * inside, -s * inside]
    a_high, a_low = split(np.concatenate(units, axis=0))
    first = np.concatenate([a_high, a_low], axis=1)

    freq = np.arange(PATCH)[None, :]
    y = np.arange(STRIDE)[:, None]
    c, s = trig(y * freq)

    def second(c, s, count):
        c, s = block_diagonal(c, count), block_diagonal(s, count)
        return split(np.block([[c, -s], [s, c]]))

    fine_w = second(c, s, LANES // STRIDE)
    coarse_w = second(np.repeat(c, 2, axis=0), np.repeat(s, 2, axis=0), LANES // (2 * STRIDE))

    shift = np.arange(WINDOW) - WINDOW // 2
    c, s = trig(np.arange(PATCH)[:, None] * shift[None, :])
    c, s = block_diagonal(c, 4), block_diagonal(s, 4)
    inverse = split(np.block([[c, s], [-s, c]]))

    weight = np.where((k == 0) | (k == PATCH // 2), 1.0, 2.0) * keep
    c, s = trig(shift[:, None] * np.arange(KP)[None, :])
    last_high, last_low = split(np.concatenate([c * weight.T, -s * weight.T], axis=1))
    last = np.concatenate([last_high, last_high, last_low], axis=1)
    energy = np.kron(np.eye(4), np.ones((PATCH, WINDOW)))
    return [
        first,
        *fine_w,
        *coarse_w,
        *inverse,
        last,
        np.asarray(energy, np.float32),
        np.asarray(np.broadcast_to(weight, (KP, LANES)), np.float32),
    ]


def split_value(value):
    high = value.astype(BF16)
    return high, (value - high.astype(F32)).astype(BF16)


def matmul(a, b):
    return jnp.dot(a, b, preferred_element_type=F32)


def section_spectra(pixels, first, fine_w, coarse_w, fine_rows, coarse_rows):
    half = matmul(first, jnp.concatenate([pixels, pixels], axis=0))
    width = half.shape[1]
    tiles = width // LANES
    row = lax.broadcasted_iota(jnp.int32, (KP, width), 0)
    fine_in, coarse_in = [], []
    for unit in range(fine_rows + coarse_rows):
        real = half[2 * KP * unit : 2 * KP * unit + KP]
        imag = half[2 * KP * unit + KP : 2 * KP * (unit + 1)]
        sums = real[0:1]
        high = sums.astype(BF16).astype(F32)
        middle = (sums - high).astype(BF16).astype(F32)
        low = sums - high - middle
        real = jnp.where(row == 0, high, real)
        real = jnp.where(row == HALF, middle, real)
        real = jnp.where(row == HALF + 1, low, real)
        target = fine_in if unit < fine_rows else coarse_in
        for tile in range(tiles):
            at = slice(LANES * tile, LANES * (tile + 1))
            target.append(jnp.concatenate([real[:, at], imag[:, at]], axis=1))

    def transform(parts, weights):
        high, low = split_value(jnp.concatenate(parts, axis=0))
        w_high, w_low = weights
        return matmul(high, w_high) + matmul(low, w_high) + matmul(high, w_low)

    fine = transform(fine_in, fine_w)
    coarse = transform(coarse_in, coarse_w)
    wide = 2 * LANES
    lane = lax.broadcasted_iota(jnp.int32, (KP, wide), 1)
    krow = lax.broadcasted_iota(jnp.int32, (KP, wide), 0)
    sign = jnp.where(lane % 2 == 0, 1.0, -1.0).astype(F32)
    dc = (krow == 0) & (lane % PATCH == 0)

    def finish(parts, rows):
        count = len(parts) // rows
        rolled = [pltpu.roll(part, wide - PATCH, 1) for part in parts]
        done = []
        for index, part in enumerate(parts):
            if index % count == count - 1:
                following = jnp.where(lane < wide - PATCH, rolled[index], 0.0)
            else:
                following = jnp.where(lane < wide - PATCH, rolled[index], rolled[index + 1])
            value = part + sign * following
            value = jnp.where(krow == 0, value + value[HALF : HALF + 1] + value[HALF + 1 : HALF + 2], value)
            value = jnp.where(dc, 0.0, value)
            done.append(value)
        return done

    def groups(offset):
        fine_parts = [
            fine[KP * g : KP * (g + 1), offset * wide : (offset + 1) * wide]
            for g in range(fine_rows * tiles)
        ]
        coarse_parts = [
            jnp.concatenate(
                [
                    coarse[KP * g : KP * (g + 1), offset * LANES : (offset + 1) * LANES],
                    coarse[KP * (g + 1) : KP * (g + 2), offset * LANES : (offset + 1) * LANES],
                ],
                axis=1,
            )
            for g in range(0, coarse_rows * tiles, 2)
        ]
        return finish(fine_parts, fine_rows) + finish(coarse_parts, coarse_rows)

    return groups(0), groups(1)


def block_transpose(value):
    row = lax.broadcasted_iota(jnp.int32, value.shape, 0) % 4
    block = lax.broadcasted_iota(jnp.int32, value.shape, 1) // WINDOW
    rows = value.shape[0]
    moved = pltpu.roll(value, 2 * WINDOW, 1)
    other = jnp.where(row < 2, pltpu.roll(moved, rows - 2, 0), pltpu.roll(moved, 2, 0))
    value = jnp.where((row // 2) == (block // 2), value, other)
    right = pltpu.roll(pltpu.roll(value, WINDOW, 1), rows - 1, 0)
    left = pltpu.roll(pltpu.roll(value, LANES - WINDOW, 1), 1, 0)
    other = jnp.where(row % 2 == 0, right, left)
    return jnp.where((row % 2) == (block % 2), value, other)


def compute(const_count, *refs):
    pixels_ref, fine_mask_ref, coarse_mask_ref = refs[:3]
    sources = refs[3 : 3 + const_count]
    maps_ref = refs[3 + const_count]
    own_ref, near_ref, far_ref, rim_ref, real_ref, imag_ref, sums_ref = refs[4 + const_count : 11 + const_count]
    held = refs[11 + const_count : 11 + 2 * const_count]
    own_sem, const_sem, send_sem, recv_sem = refs[11 + 2 * const_count :]
    sec, strip = lax.axis_index("sec"), lax.axis_index("strip")
    secs, strips = lax.axis_size("sec"), lax.axis_size("strip")

    own_copy = pltpu.make_async_copy(pixels_ref.at[0], own_ref, own_sem)
    own_copy.start()
    const_copies = [
        pltpu.make_async_copy(source, target, const_sem.at[index])
        for index, (source, target) in enumerate(zip(sources, held))
    ]
    for copy in const_copies:
        copy.start()

    barrier = pltpu.get_barrier_semaphore()

    def greet(condition, device):
        @pl.when(condition)
        def _():
            pl.semaphore_signal(barrier, inc=1, device_id=device, device_id_type=MESH)

    greet(sec + 1 < secs, {"sec": sec + 1})
    greet(strip + 1 < strips, {"strip": strip + 1})
    targets = lax.min(sec, 1) + lax.min(strip, 1)

    @pl.when(targets >= 1)
    def _():
        pl.semaphore_wait(barrier, targets)

    piece = pixels_ref.shape[1] // CHUNKS

    def remote(source, target, flow, chunk, device):
        rows = pl.ds(piece * chunk, piece)
        return pltpu.make_async_remote_copy(
            src_ref=source.at[rows],
            dst_ref=target.at[rows],
            send_sem=send_sem.at[flow, chunk],
            recv_sem=recv_sem.at[flow, chunk],
            device_id=device,
            device_id_type=MESH,
        )

    above, before = {"strip": strip - 1}, {"sec": sec - 1}
    rim_copies = [
        [remote(source, rim_ref.at[index], index, c, above) for c in range(CHUNKS)]
        for index, source in enumerate((pixels_ref.at[0], near_ref, far_ref))
    ]
    near_copies = [remote(pixels_ref.at[0], near_ref, 3, c, before) for c in range(CHUNKS)]
    far_copies = [remote(near_ref, far_ref, 4, c, before) for c in range(CHUNKS)]
    up = strip >= 1
    below = strip + 1 < strips
    has_near, has_far = sec + 1 < secs, sec + 2 < secs

    def each(condition, copies, method):
        @pl.when(condition)
        def _():
            for copy in copies:
                getattr(copy, method)()

    for c in range(CHUNKS):
        pl.when(up)(rim_copies[0][c].start)
        pl.when(sec >= 1)(near_copies[c].start)

    def fill(condition, ref, *index):
        @pl.when(condition)
        def _():
            ref[index if index else ...] = jnp.zeros(ref.shape[len(index) :], ref.dtype)

    for d in range(3):
        fill(jnp.logical_not(below & (sec + d < secs)), rim_ref, d)
    fill(sec + 1 >= secs, near_ref)
    fill(sec + 2 >= secs, far_ref)
    sums_ref[...] = jnp.zeros_like(sums_ref)

    fine_rows, fine_cols = fine_mask_ref.shape[1:]
    coarse_rows, coarse_cols = coarse_mask_ref.shape[1:]
    count = (fine_rows * fine_cols + coarse_rows * coarse_cols) // 4
    (
        first_ref,
        fine_high_ref,
        fine_low_ref,
        coarse_high_ref,
        coarse_low_ref,
        inverse_high_ref,
        inverse_low_ref,
        last_ref,
        energy_ref,
        weight_ref,
    ) = held

    def spread(mask, cols):
        source = lax.broadcasted_iota(jnp.int32, (cols, cols * WINDOW), 0)
        target = lax.broadcasted_iota(jnp.int32, (cols, cols * WINDOW), 1) // WINDOW
        picks = jnp.where(source == target, 1.0, 0.0).astype(BF16)
        return matmul(mask.astype(F32).astype(BF16), picks)

    fine_mask = spread(fine_mask_ref[0], fine_cols)
    coarse_mask = spread(coarse_mask_ref[0], coarse_cols)
    masks = [
        m[r : r + 1, LANES * t : LANES * (t + 1)]
        for m in (fine_mask, coarse_mask)
        for r in range(m.shape[0])
        for t in range(m.shape[1] // LANES)
    ]
    scales = []

    def analyse(section, main_ref):
        each(below & (sec + section < secs), rim_copies[section], "wait_recv")
        weight = jnp.concatenate([weight_ref[...]] * 2, axis=1)
        real, imag = section_spectra(
            jnp.concatenate([main_ref[...], rim_ref[section]], axis=0),
            first_ref[...],
            (fine_high_ref[...], fine_low_ref[...]),
            (coarse_high_ref[...], coarse_low_ref[...]),
            fine_rows,
            coarse_rows,
        )
        for g in range(count):
            real_ref[section, KP * g : KP * (g + 1)] = real[g]
            imag_ref[section, KP * g : KP * (g + 1)] = imag[g]
            power = weight * (real[g] * real[g] + imag[g] * imag[g])
            sums_ref[section, g : g + 1] = jnp.sum(power, axis=0, keepdims=True)
        total = jnp.dot(
            sums_ref[section], energy_ref[...], preferred_element_type=F32, precision=lax.Precision.HIGHEST
        )
        scales.append(1.0 / jnp.sqrt(total * (1.0 / float(PATCH) ** 4) + 1e-05))

    def correlate(d):
        cross_real = real_ref[0] * real_ref[d] + imag_ref[0] * imag_ref[d]
        cross_imag = real_ref[0] * imag_ref[d] - imag_ref[0] * real_ref[d]
        cross = jnp.concatenate([cross_real.astype(BF16), cross_imag.astype(BF16)], axis=1)
        rows = matmul(cross, inverse_high_ref[...]) + matmul(cross, inverse_low_ref[...])
        stacked = []
        for g in range(count):
            part = rows[KP * g : KP * (g + 1)]
            stacked.append(jnp.concatenate([part[:, :LANES], part[:, LANES:]], axis=0))
        high, low = split_value(jnp.concatenate(stacked, axis=1))
        maps = matmul(last_ref[...], jnp.concatenate([high, low, high], axis=0))
        for g in range(count):
            scale = scales[0][g : g + 1] * scales[d][g : g + 1] * masks[g] * (1.0 / float(PATCH) ** 3)
            maps_ref[d - 1, g] = block_transpose(maps[:, LANES * g : LANES * (g + 1)] * scale)

    @pl.when(has_near)
    def _():
        for c in range(CHUNKS):
            near_copies[c].wait_recv()
            pl.when(up)(rim_copies[1][c].start)
            pl.when(sec >= 1)(far_copies[c].start)

    own_copy.wait()
    for copy in const_copies:
        copy.wait()
    analyse(0, own_ref)

    @pl.when(has_far)
    def _():
        for c in range(CHUNKS):
            far_copies[c].wait_recv()
            pl.when(up)(rim_copies[2][c].start)

    analyse(1, near_ref)
    correlate(1)
    analyse(2, far_ref)
    correlate(2)
    each(sec >= 1, near_copies, "wait_send")
    each(has_near & (sec >= 1), far_copies, "wait_send")
    each(up, rim_copies[0], "wait_send")
    each(has_near & up, rim_copies[1], "wait_send")
    each(has_far & up, rim_copies[2], "wait_send")


def arrange(maps_ref, fine_out_ref, coarse_out_ref):
    fine_rows, fine_cols = fine_out_ref.shape[2:4]
    coarse_rows, coarse_cols = coarse_out_ref.shape[2:4]
    fine_groups = fine_rows * fine_cols // 4
    count = fine_groups + coarse_rows * coarse_cols // 4
    for d in range(1):
        for g in range(count):
            value = maps_ref[d, g]
            if g < fine_groups:
                ref, local_g, cols = fine_out_ref, g, fine_cols
            else:
                ref, local_g, cols = coarse_out_ref, g - fine_groups, coarse_cols
            i, j = divmod(4 * local_g, cols)
            for q in range(WINDOW // 4):
                ref[0, d, i, j : j + 4, LANES * q : LANES * (q + 1)] = value[4 * q : 4 * (q + 1)]


def local(sections, mask_fine, mask_coarse):
    strip_rows, width = sections.shape[1:]
    consts = [jnp.asarray(t) for t in tables(strip_rows)]
    fine_rows, fine_cols = mask_fine.shape[1:]
    coarse_rows, coarse_cols = mask_coarse.shape[1:]
    count = (fine_rows * fine_cols + coarse_rows * coarse_cols) // 4
    vmem = pl.BlockSpec(memory_space=pltpu.VMEM)
    anywhere = pl.BlockSpec(memory_space=pl.ANY)
    flat = WINDOW * WINDOW
    maps = pl.pallas_call(
        functools.partial(compute, len(consts)),
        out_shape=jax.ShapeDtypeStruct((2, count, WINDOW, LANES), F32),
        in_specs=[anywhere, vmem, vmem] + [anywhere] * len(consts),
        out_specs=vmem,
        scratch_shapes=[
            pltpu.VMEM((strip_rows, width), BF16),
            pltpu.VMEM((strip_rows, width), BF16),
            pltpu.VMEM((strip_rows, width), BF16),
            pltpu.VMEM((3, strip_rows, width), BF16),
            pltpu.VMEM((3, KP * count, 2 * LANES), F32),
            pltpu.VMEM((3, KP * count, 2 * LANES), F32),
            pltpu.VMEM((3, -(-count // 8) * 8, 2 * LANES), F32),
            *[pltpu.VMEM(c.shape, c.dtype) for c in consts],
            pltpu.SemaphoreType.DMA,
            pltpu.SemaphoreType.DMA((len(consts),)),
            pltpu.SemaphoreType.DMA((5, CHUNKS)),
            pltpu.SemaphoreType.DMA((5, CHUNKS)),
        ],
        compiler_params=pltpu.CompilerParams(collective_id=0, has_side_effects=True),
    )(sections, mask_fine, mask_coarse, *consts)
    return pl.pallas_call(
        arrange,
        out_shape=(
            jax.ShapeDtypeStruct((1, 2, fine_rows, fine_cols, flat), F32),
            jax.ShapeDtypeStruct((1, 2, coarse_rows, coarse_cols, flat), F32),
        ),
        grid=(2,),
        in_specs=[pl.BlockSpec((1, count, WINDOW, LANES), lambda d: (d, 0, 0, 0))],
        out_specs=(
            pl.BlockSpec((1, 1, fine_rows, fine_cols, flat), lambda d: (0, d, 0, 0, 0)),
            pl.BlockSpec((1, 1, coarse_rows, coarse_cols, flat), lambda d: (0, d, 0, 0, 0)),
        ),
    )(maps)


def solution(mesh):
    in_specs = (
        P("sec", "strip", "groups"),
        P("sec", "strip", "groups"),
        P("sec", "strip", "groups"),
    )
    out_specs = (P("sec", None, "strip", "groups", None), P("sec", None, "strip", "groups", None))
    return jax.shard_map(local, mesh=mesh, in_specs=in_specs, out_specs=out_specs, check_vma=False)
```
